256 devices in a mesh: param: 16 (over y_lo, x, core), proj: 16 (over y_hi, z).
Axes of the slice: x: 4, y: 4 (y_hi: 2, y_lo: 2; y = y_hi * 2 + y_lo), z: 8, core: 2. Of those that a mesh axis runs over, the one named last changes fastest.
Arguments:
- query_grads: float32 [256, 131072], P(None, 'param'), may hold values from -45 to 45, as said below
- stored: float32 [16384, 16384], P('param', 'proj'), may hold values from -6 to 6
- proj_seed: int32 [2], replicated, may hold values from 0 to 32748
- offsets: int32 [16], P('param'), may hold values from 0 to 32748
Outputs:
- similarity: float32 [256, 16384], P('proj', 'param')
The draws below stay inside these ranges and needn't reach their ends.
Inputs may be any that keep to these rules, and one draw needn't show every extreme that they name: `query_grads`: query gradients have row and coordinate scales that differ.
All inputs are finite; a program needn't handle non-finite values.
Results may differ from the reference program's by a relative error of at most 0.0003.
Values sent between devices are 32-bit elements; how exact they have to be, the bound alone decides.
No kernel may reach another device: no remote copies, remote signals or barrier semaphores. Data moves between devices by JAX's collectives and lax.ppermute only.
A program may use at most 128 MiB of HBM per device.

```python
import math
import jax
import jax.numpy as jnp
from jax import lax

QUERIES = 256
PARAMS = 131072
PWIDTH = 16384
STORE = 16384
N_PARAM = 16
N_PROJ = 16


def draw_query_grads(key, part):
    keys = jax.random.split(key, 3)
    row_scale = jnp.exp(jax.random.uniform(keys[0], (QUERIES, 1), jnp.float32) * math.log(10.0))
    column_scale = jnp.exp(jax.random.uniform(keys[1], (1, PARAMS), jnp.float32) * math.log(10.0))
    values = jax.random.truncated_normal(keys[2], -4.0, 4.0, (QUERIES, PARAMS), jnp.float32)
    return values * row_scale * column_scale / 10.0


def set_ends(array, key, least, high):
    extent = array.shape
    spot = [jax.random.randint(jax.random.fold_in(key, axis), (), 0, extent[axis]) for axis in range(len(extent))]
    array = array.at[tuple(spot)].set(least)
    longest = extent.index(max(extent))
    spot[longest] = (spot[longest] + 1) % extent[longest]
    return array.at[tuple(spot)].set(high)


def block_levels(stream_key, dims, shards, low, largest):
    def one(dim, shards_of):
        heights = jax.random.uniform(jax.random.fold_in(jax.random.fold_in(stream_key, 6), dim), (shards_of,), jnp.float32, low / len(shards), largest / len(shards))
        return jnp.repeat(jnp.exp(heights), dims[dim] // shards_of).reshape((-1,) + (1,) * (len(dims) - dim - 1))

    loudness = one(*shards[0])
    for cut in shards[1:]:
        loudness = loudness * one(*cut)
    return loudness


def gaussian(rng, shape, width, most, shards=(), kind=jnp.bfloat16):
    array = jax.random.normal(rng, shape, jnp.float32) * width
    if len(shards) > 0:
        array = block_levels(rng, shape, shards, -0.22, 0.18) * array
    return jnp.clip(array, min=-most, max=most).astype(kind)


def setup_inputs(seed: int = 0) -> dict:
    key_list = jax.random.split(jax.random.key(seed), 5)
    return {
        "query_grads": draw_query_grads(jax.random.fold_in(key_list[4], 71), 0),
        "stored": gaussian(key_list[1], (STORE, PWIDTH), 1.0, 6.0, ((0, 16), (1, 16)), jnp.float32),
        "proj_seed": jax.random.randint(key_list[2], (2,), 0, 32749).astype(jnp.int32),
        "offsets": set_ends(jax.random.randint(key_list[3], (N_PARAM,), 0, 32749), jax.random.fold_in(key_list[3], 1), 0, 32748).astype(jnp.int32),
    }


modulus = 32749
epsilon = 1e-06

def proj_tile(offset, proj_seed, column_start, coords_count, width_count, param_total, width_total):
    coord_ids = jnp.arange(coords_count, dtype=jnp.int32)[:, None] + offset
    column_ids = column_start + jnp.arange(width_count, dtype=jnp.int32)[None, :]
    coord_hash = (coord_ids * 1103 + proj_seed[0]) % modulus
    column_hash = (column_ids * 2111 + proj_seed[1]) % modulus
    mixed = (coord_hash * column_hash + coord_hash + 3 * column_hash + 17) % modulus
    mixed = (mixed * mixed + coord_hash) % modulus
    uniform_val = (mixed.astype(jnp.float32) + 0.5) * (2.0 / modulus) - 1.0
    column_gain = jnp.sqrt(1.0 + 2.0 * column_ids.astype(jnp.float32) / width_total)
    return uniform_val * column_gain * math.sqrt(3.0 / param_total)

def reference(query_grads, stored, proj_seed, offsets):
    queries, param_total = query_grads.shape
    blocks = offsets.shape[0]
    coords_dev = param_total // blocks
    width_total = stored.shape[1]
    width_dev = width_total // N_PROJ

    def column_block(column_index):
        column_start = column_index * width_dev

        def add_block(accum, block_id):
            piece = proj_tile(offsets[block_id], proj_seed, column_start, coords_dev, width_dev, param_total, width_total)
            grads = lax.dynamic_slice_in_dim(query_grads, block_id * coords_dev, coords_dev, 1)
            return (accum + jnp.dot(grads, piece, precision=lax.Precision.HIGHEST, preferred_element_type=jnp.float32), None)
        accum, _ = lax.scan(add_block, jnp.zeros((queries, width_dev), jnp.float32), jnp.arange(blocks, dtype=jnp.int32))
        return accum
    stacked = lax.map(column_block, jnp.arange(N_PROJ, dtype=jnp.int32))
    projected = jnp.transpose(stacked, (1, 0, 2)).reshape(queries, width_total)
    inverse = lax.rsqrt(lax.optimization_barrier(jnp.mean(projected * projected, axis=1, keepdims=True)) + epsilon)
    raw_scores = lax.dot_general(projected, stored, (((1,), (1,)), ((), ())), precision=lax.Precision.HIGHEST, preferred_element_type=jnp.float32)
    return jnp.tanh(raw_scores * inverse / math.sqrt(width_total))
```

```python
import functools
import math

import jax
import jax.numpy as jnp
from jax import lax
from jax.experimental import pallas as pl
from jax.experimental.pallas import tpu as pltpu
from jax.sharding import PartitionSpec as P

modulus = 32749
epsilon = 1e-06
turn_whole = 2**32 // modulus
turn_rest = 2**32 / modulus - turn_whole
tile = 256
NT = (((1,), (1,)), ((), ()))
bf16 = jnp.bfloat16


def reduced(x):
    quotient = (x.astype(jnp.float32) * (1.0 / modulus)).astype(jnp.int32)
    rest = x - quotient * modulus
    rest = jnp.where(rest < 0, rest + modulus, rest)
    return jnp.where(rest >= modulus, rest - modulus, rest)


def turns(residue):
    return residue * turn_whole + jnp.round(residue.astype(jnp.float32) * turn_rest).astype(jnp.int32)


def halves(x):
    high = x.astype(bf16)
    return high, (x - high.astype(jnp.float32)).astype(bf16)


def product(a, b):
    return lax.dot_general(a, b, NT, preferred_element_type=jnp.float32)


def quadratic_start(seed_ref, offset_ref, column_start, coord_start, lanes):
    coord = lax.broadcasted_iota(jnp.int32, (8, lanes), 1) + (coord_start + offset_ref[0])
    column = lax.broadcasted_iota(jnp.int32, (8, lanes), 0) + column_start
    a = reduced(coord * 1103 + seed_ref[0]) + 3
    b = reduced(column * 2111 + seed_ref[1]) + 1
    w = reduced(a * b + 14)
    step = reduced(a * (8 * 2111))
    square = reduced(step * step)
    phase = turns(reduced(w * w + (a - 3))) + (turn_whole // 2 - 2**31)
    first = turns(reduced(2 * reduced(w * step) + square))
    second = turns(reduced(2 * square))
    return phase, first, second


def project_body(seed_ref, offset_ref, grads_ref, mine_ref, send_ref, even0, even1, odd0, odd1, total, *, width, steps, scale, width_total):
    step = pl.program_id(0)
    column_start = lax.axis_index("proj") * width
    core = lax.axis_index("param") % 2

    def generate(coord_start, high_ref, low_ref):
        phase, first, second = quadratic_start(seed_ref, offset_ref, column_start, coord_start, tile)
        for row in range(0, width, 16):
            rows = []
            for _ in range(2):
                rows.append(phase)
                phase = phase + first
                first = first + second
            high, low = halves(jnp.concatenate(rows, 0).astype(jnp.float32))
            high_ref[row : row + 16, :] = high
            low_ref[row : row + 16, :] = low

    def multiply(high_ref, low_ref, grads):
        g0, g1 = halves(grads)
        p0, p1 = high_ref[...], low_ref[...]
        total[...] += product(p0, g0) + (product(p0, g1) + product(p1, g0))

    @pl.when(step == 0)
    def _():
        total[...] = jnp.zeros_like(total)
        generate(0, even0, even1)

    start = step * (2 * tile)
    generate(start + tile, odd0, odd1)
    multiply(even0, even1, grads_ref[:, :tile])
    generate(start + 2 * tile, even0, even1)
    multiply(odd0, odd1, grads_ref[:, tile:])

    @pl.when(step == steps - 1)
    def _():
        column = lax.broadcasted_iota(jnp.int32, (width, 1), 0) + column_start
        gain = jnp.sqrt(1.0 + 2.0 * column.astype(jnp.float32) / width_total) * (scale * 2.0**-31)
        left = total[:, :128] * gain
        right = total[:, 128:] * gain
        mine_ref[...] = jnp.where(core == 0, left, right)
        send_ref[...] = jnp.where(core == 0, right, left)


def project(seed, offsets, grads, width, param_total, width_total):
    queries, coords = grads.shape
    steps = coords // (2 * tile)
    half = jax.ShapeDtypeStruct((width, queries // 2), jnp.float32)
    out_spec = pl.BlockSpec((width, queries // 2), lambda i: (0, 0))
    return pl.pallas_call(
        functools.partial(project_body, width=width, steps=steps, scale=math.sqrt(3.0 / param_total), width_total=width_total),
        grid=(steps,),
        in_specs=[
            pl.BlockSpec(memory_space=pltpu.SMEM),
            pl.BlockSpec(memory_space=pltpu.SMEM),
            pl.BlockSpec((queries, 2 * tile), lambda i: (0, i)),
        ],
        out_specs=[out_spec, out_spec],
        out_shape=[half, half],
        scratch_shapes=[pltpu.VMEM((width, tile), bf16)] * 4 + [pltpu.VMEM((width, queries), jnp.float32)],
        compiler_params=pltpu.CompilerParams(
            dimension_semantics=("arbitrary",),
            vmem_limit_bytes=48 << 20,
        ),
        name="project",
    )(seed, offsets, grads)


def copies_body(parts_ref, copies_ref):
    own = parts_ref[0]
    for i in range(1, parts_ref.shape[0]):
        own += parts_ref[i]
    own = own.T
    for i in range(parts_ref.shape[0]):
        copies_ref[i] = own


def summed_copies(parts):
    peers, rows, cols = parts.shape
    return pl.pallas_call(
        copies_body, out_shape=jax.ShapeDtypeStruct((peers, cols, rows), parts.dtype), name="summed_copies"
    )(parts)


def score_body(own_ref, other_ref, stored_ref, keep_ref, send_ref, high, low, *, blocks):
    step = pl.program_id(0)
    same = (lax.axis_index("param") % 2) == (lax.axis_index("proj") // 8)

    @pl.when(step == 0)
    def _():
        for side, out_ref in ((0, keep_ref), (1, send_ref)):
            squares = jnp.zeros((128, 128), jnp.float32)
            for b in range(8):
                own, other = own_ref[b], other_ref[b]
                value = jnp.where(same, own, other) if side == 0 else jnp.where(same, other, own)
                h, l = halves(value)
                high[128 * side : 128 * side + 128, 128 * b : 128 * b + 128] = h
                low[128 * side : 128 * side + 128, 128 * b : 128 * b + 128] = l
                squares += value * value
            sums = jnp.broadcast_to(jnp.sum(squares, axis=1, keepdims=True), (128, 128))
            lane = lax.broadcasted_iota(jnp.int32, (8, 128), 1)
            for z in range(8):
                out_ref[z, 128:, :] = jnp.where(lane < 64, sums[16 * z : 16 * z + 8], sums[16 * z + 8 : 16 * z + 16])

    s0, s1 = halves(stored_ref[...])
    p0, p1 = high[...], low[...]
    left = jnp.concatenate([p0, p1, p0], 1)
    right = jnp.concatenate([s0, s0, s1], 1)
    raw = product(left, right)
    for side, out_ref in ((0, keep_ref), (1, send_ref)):
        for c in range(blocks):
            for z in range(8):
                row = 128 * side + 16 * z
                out_ref[z, pl.ds((step * blocks + c) * 16, 16), :] = raw[row : row + 16, 128 * c : 128 * c + 128]


def scores(own, other, stored):
    rows, width = stored.shape
    blocks = 2
    out = jax.ShapeDtypeStruct((8, rows // 8 + 8, 128), jnp.float32)
    whole = pl.BlockSpec((8, 128, 128), lambda i: (0, 0, 0))
    out_spec = pl.BlockSpec(out.shape, lambda i: (0, 0, 0))
    return pl.pallas_call(
        functools.partial(score_body, blocks=blocks),
        grid=(rows // (128 * blocks),),
        in_specs=[whole, whole, pl.BlockSpec((128 * blocks, width), lambda i: (i, 0))],
        out_specs=[out_spec, out_spec],
        out_shape=[out, out],
        scratch_shapes=[pltpu.VMEM((256, width), bf16)] * 2,
        compiler_params=pltpu.CompilerParams(dimension_semantics=("arbitrary",), vmem_limit_bytes=48 << 20),
        name="scores",
    )(own, other, stored)


def finish_body(parts_ref, out_ref, *, width_total):
    total = parts_ref[0]
    for i in range(1, 8):
        total += parts_ref[i]
    tail = total[128:]
    sums = jnp.concatenate([tail[:, :1], tail[:, 64:65]], 0)
    factor = lax.rsqrt(sums / width_total + epsilon) * (1.0 / math.sqrt(width_total))
    for c in range(8):
        out_ref[:, 128 * c : 128 * c + 128] = jnp.tanh(total[16 * c : 16 * c + 16] * factor)


def finish(parts, width_total):
    return pl.pallas_call(
        functools.partial(finish_body, width_total=width_total),
        out_shape=jax.ShapeDtypeStruct((16, 1024), jnp.float32),
        name="finish",
    )(parts)


core_swap = [(i, i ^ 1) for i in range(16)]
y_swap = [(i, i ^ 8) for i in range(16)]
chips = [[c + 2 * i for i in range(8)] for c in range(2)]
rings = [[8 * y + z for z in range(8)] for y in range(2)]


def exchanged(x, axis, groups):
    return lax.all_to_all(x, axis, 0, 0, axis_index_groups=groups, tiled=True)


def on_device(query_grads, stored, proj_seed, offsets):
    width = stored.shape[1]
    param_total = query_grads.shape[1] * 16
    width_total = width * 16
    mine, send = project(proj_seed, offsets, query_grads, width, param_total, width_total)
    part = (mine + lax.ppermute(send, "param", core_swap)).reshape(8, width // 8, 128)
    own = exchanged(summed_copies(exchanged(part, "param", chips)), "param", chips)
    other = lax.ppermute(own, "param", core_swap)
    keep, give = scores(own, other, stored)
    half = keep + lax.ppermute(give, "proj", y_swap)
    return finish(exchanged(half, "proj", rings), width_total)


def solution(mesh):
    placed = (P(None, "param"), P("param", "proj"), P(), P("param"))
    return jax.shard_map(on_device, mesh=mesh, in_specs=placed, out_specs=P("proj", "param"), check_vma=False)
```

```python
import functools
import math

import jax
import jax.numpy as jnp
from jax import lax
from jax.experimental import pallas as pl
from jax.experimental.pallas import tpu as pltpu
from jax.sharding import PartitionSpec as P

modulus = 32749
epsilon = 1e-06
turn_whole = 2**32 // modulus
turn_rest = 2**32 / modulus - turn_whole
tile = 256
NT = (((1,), (1,)), ((), ()))
bf16 = jnp.bfloat16


def reduced(x):
    quotient = (x.astype(jnp.float32) * (1.0 / modulus)).astype(jnp.int32)
    rest = x - quotient * modulus
    rest = jnp.where(rest < 0, rest + modulus, rest)
    return jnp.where(rest >= modulus, rest - modulus, rest)


def turns(residue):
    return residue * turn_whole + jnp.round(residue.astype(jnp.float32) * turn_rest).astype(jnp.int32)


def halves(x):
    high = x.astype(bf16)
    return high, (x - high.astype(jnp.float32)).astype(bf16)


def product(a, b):
    return lax.dot_general(a, b, NT, preferred_element_type=jnp.float32)


def quadratic_start(seed_ref, offset_ref, column_start, coord_start, lanes):
    coord = lax.broadcasted_iota(jnp.int32, (8, lanes), 1) + (coord_start + offset_ref[0])
    column = lax.broadcasted_iota(jnp.int32, (8, lanes), 0) + column_start
    a = reduced(coord * 1103 + seed_ref[0]) + 3
    b = reduced(column * 2111 + seed_ref[1]) + 1
    w = reduced(a * b + 14)
    step = reduced(a * (8 * 2111))
    square = reduced(step * step)
    phase = turns(reduced(w * w + (a - 3))) + (turn_whole // 2 - 2**31)
    first = turns(reduced(2 * reduced(w * step) + square))
    second = turns(reduced(2 * square))
    return phase, first, second


def project_body(seed_ref, offset_ref, grads_ref, mine_ref, send_ref, even0, even1, odd0, odd1, total, *, width, steps):
    step = pl.program_id(0)
    column_start = lax.axis_index("proj") * width
    core = lax.axis_index("param") % 2

    def generate(coord_start, high_ref, low_ref):
        phase, first, second = quadratic_start(seed_ref, offset_ref, column_start, coord_start, tile)
        for row in range(0, width, 16):
            rows = []
            for _ in range(2):
                rows.append(phase)
                phase = phase + first
                first = first + second
            high, low = halves(jnp.concatenate(rows, 0).astype(jnp.float32))
            high_ref[row : row + 16, :] = high
            low_ref[row : row + 16, :] = low

    def multiply(high_ref, low_ref, grads):
        g0, g1 = halves(grads)
        p0, p1 = high_ref[...], low_ref[...]
        total[...] += product(p0, g0) + (product(p0, g1) + product(p1, g0))

    @pl.when(step == 0)
    def _():
        total[...] = jnp.zeros_like(total)
        generate(0, even0, even1)

    start = step * (2 * tile)
    generate(start + tile, odd0, odd1)
    multiply(even0, even1, grads_ref[:, :tile])
    generate(start + 2 * tile, even0, even1)
    multiply(odd0, odd1, grads_ref[:, tile:])

    @pl.when(step == steps - 1)
    def _():
        left, right = total[:, :128], total[:, 128:]
        mine_ref[...] = jnp.where(core == 0, left, right)
        send_ref[...] = jnp.where(core == 0, right, left)


def project(seed, offsets, grads, width):
    queries, coords = grads.shape
    steps = coords // (2 * tile)
    half = jax.ShapeDtypeStruct((width, queries // 2), jnp.float32)
    out_spec = pl.BlockSpec((width, queries // 2), lambda i: (0, 0))
    return pl.pallas_call(
        functools.partial(project_body, width=width, steps=steps),
        grid=(steps,),
        in_specs=[
            pl.BlockSpec(memory_space=pltpu.SMEM),
            pl.BlockSpec(memory_space=pltpu.SMEM),
            pl.BlockSpec((queries, 2 * tile), lambda i: (0, i)),
        ],
        out_specs=[out_spec, out_spec],
        out_shape=[half, half],
        scratch_shapes=[pltpu.VMEM((width, tile), bf16)] * 4 + [pltpu.VMEM((width, queries), jnp.float32)],
        compiler_params=pltpu.CompilerParams(
            dimension_semantics=("arbitrary",),
            vmem_limit_bytes=48 << 20,
        ),
        name="project",
    )(seed, offsets, grads)


def copies_body(parts_ref, copies_ref, *, scale, width, width_total):
    own = parts_ref[0]
    for i in range(1, parts_ref.shape[0]):
        own += parts_ref[i]
    own = own.T
    chip = lax.axis_index("param") // 2
    column = lax.broadcasted_iota(jnp.int32, (1, 128), 1) + (lax.axis_index("proj") * width + chip * 128)
    own = own * (jnp.sqrt(1.0 + 2.0 * column.astype(jnp.float32) / width_total) * (scale * 2.0**-31))
    for i in range(parts_ref.shape[0]):
        copies_ref[i] = own


def whole(shape):
    return pl.BlockSpec(shape, lambda i: (0,) * len(shape))


def summed_copies(parts, param_total, width, width_total):
    peers, rows, cols = parts.shape
    return pl.pallas_call(
        functools.partial(copies_body, scale=math.sqrt(3.0 / param_total), width=width, width_total=width_total),
        grid=(1,),
        in_specs=[whole(parts.shape)],
        out_specs=whole((peers, cols, rows)),
        out_shape=jax.ShapeDtypeStruct((peers, cols, rows), parts.dtype),
        compiler_params=pltpu.CompilerParams(vmem_limit_bytes=8 << 20),
        name="summed_copies",
    )(parts)


def score_body(own_ref, other_ref, stored_ref, out_ref, high, low, *, blocks):
    step = pl.program_id(0)
    first = lax.axis_index("param") % 2 == 0

    @pl.when(step == 0)
    def _():
        for side in range(2):
            squares = jnp.zeros((128, 128), jnp.float32)
            for b in range(8):
                own, other = own_ref[b], other_ref[b]
                value = jnp.where(first, own, other) if side == 0 else jnp.where(first, other, own)
                h, l = halves(value)
                high[128 * side : 128 * side + 128, 128 * b : 128 * b + 128] = h
                low[128 * side : 128 * side + 128, 128 * b : 128 * b + 128] = l
                squares += value * value
            sums = jnp.broadcast_to(jnp.sum(squares, axis=1, keepdims=True), (128, 128))
            lane = lax.broadcasted_iota(jnp.int32, (8, 128), 1)
            for z in range(8):
                out_ref[8 * side + z, 128:, :] = jnp.where(lane < 64, sums[16 * z : 16 * z + 8], sums[16 * z + 8 : 16 * z + 16])

    s0, s1 = halves(stored_ref[...])
    p0, p1 = high[...], low[...]
    left = jnp.concatenate([p0, p1, p0], 1)
    right = jnp.concatenate([s0, s0, s1], 1)
    raw = product(left, right)
    for c in range(blocks):
        for peer in range(16):
            out_ref[peer, pl.ds((step * blocks + c) * 16, 16), :] = raw[16 * peer : 16 * peer + 16, 128 * c : 128 * c + 128]


def scores(own, other, stored):
    rows, width = stored.shape
    blocks = 2
    out = jax.ShapeDtypeStruct((16, rows // 8 + 8, 128), jnp.float32)
    return pl.pallas_call(
        functools.partial(score_body, blocks=blocks),
        grid=(rows // (128 * blocks),),
        in_specs=[whole(own.shape), whole(other.shape), pl.BlockSpec((128 * blocks, width), lambda i: (i, 0))],
        out_specs=whole(out.shape),
        out_shape=out,
        scratch_shapes=[pltpu.VMEM((256, width), bf16)] * 2,
        compiler_params=pltpu.CompilerParams(dimension_semantics=("arbitrary",), vmem_limit_bytes=48 << 20),
        name="scores",
    )(own, other, stored)


def finish_body(parts_ref, out_ref, *, width_total):
    total = parts_ref[0]
    for i in range(1, 16):
        total += parts_ref[i]
    tail = total[128:]
    sums = jnp.concatenate([tail[:, :1], tail[:, 64:65]], 0)
    factor = lax.rsqrt(sums / width_total + epsilon) * (1.0 / math.sqrt(width_total))
    for c in range(8):
        out_ref[:, 128 * c : 128 * c + 128] = jnp.tanh(total[16 * c : 16 * c + 16] * factor)


def finish(parts, width_total):
    return pl.pallas_call(
        functools.partial(finish_body, width_total=width_total),
        grid=(1,),
        in_specs=[whole(parts.shape)],
        out_specs=whole((16, 1024)),
        out_shape=jax.ShapeDtypeStruct((16, 1024), jnp.float32),
        compiler_params=pltpu.CompilerParams(vmem_limit_bytes=8 << 20),
        name="finish",
    )(parts)


core_swap = [(i, i ^ 1) for i in range(16)]
chips = [[c + 2 * i for i in range(8)] for c in range(2)]


def exchanged(x, axis, groups=None):
    return lax.all_to_all(x, axis, 0, 0, axis_index_groups=groups, tiled=True)


def on_device(query_grads, stored, proj_seed, offsets):
    width = stored.shape[1]
    param_total = query_grads.shape[1] * 16
    width_total = width * 16
    mine, send = project(proj_seed, offsets, query_grads, width)
    part = (mine + lax.ppermute(send, "param", core_swap)).reshape(8, width // 8, 128)
    copies = summed_copies(exchanged(part, "param", chips), param_total, width, width_total)
    own = exchanged(copies, "param", chips)
    other = lax.ppermute(own, "param", core_swap)
    return finish(exchanged(scores(own, other, stored), "proj"), width_total)


def solution(mesh):
    placed = (P(None, "param"), P("param", "proj"), P(), P("param"))
    return jax.shard_map(on_device, mesh=mesh, in_specs=placed, out_specs=P("proj", "param"), check_vma=False)
```

```python
import functools
import math

import jax
import jax.numpy as jnp
from jax import lax
from jax.experimental import pallas as pl
from jax.experimental.pallas import tpu as pltpu
from jax.sharding import PartitionSpec as P

modulus = 32749
epsilon = 1e-06
turn_whole = 2**32 // modulus
turn_rest = 2**32 / modulus - turn_whole
tile = 256
NT = (((1,), (1,)), ((), ()))
bf16 = jnp.bfloat16


def reduced(x):
    quotient = (x.astype(jnp.float32) * (1.0 / modulus)).astype(jnp.int32)
    rest = x - quotient * modulus
    rest = jnp.where(rest < 0, rest + modulus, rest)
    return jnp.where(rest >= modulus, rest - modulus, rest)


def turns(residue):
    return residue * turn_whole + jnp.round(residue.astype(jnp.float32) * turn_rest).astype(jnp.int32)


def halves(x):
    high = x.astype(bf16)
    return high, (x - high.astype(jnp.float32)).astype(bf16)


def product(a, b):
    return lax.dot_general(a, b, NT, preferred_element_type=jnp.float32)


def quadratic_start(seed_ref, offset_ref, column_start, coord_start, lanes):
    coord = lax.broadcasted_iota(jnp.int32, (8, lanes), 1) + (coord_start + offset_ref[0])
    column = lax.broadcasted_iota(jnp.int32, (8, lanes), 0) + column_start
    a = reduced(coord * 1103 + seed_ref[0]) + 3
    b = reduced(column * 2111 + seed_ref[1]) + 1
    w = reduced(a * b + 14)
    step = reduced(a * (8 * 2111))
    square = reduced(step * step)
    phase = turns(reduced(w * w + (a - 3))) + (turn_whole // 2 - 2**31)
    first = turns(reduced(2 * reduced(w * step) + square))
    second = turns(reduced(2 * square))
    return phase, first, second


def project_body(seed_ref, offset_ref, grads_ref, mine_ref, send_ref, even0, even1, odd0, odd1, total, *, width, steps):
    step = pl.program_id(0)
    column_start = lax.axis_index("proj") * width
    core = lax.axis_index("param") % 2

    def generate(coord_start, high_ref, low_ref):
        phase, first, second = quadratic_start(seed_ref, offset_ref, column_start, coord_start, tile)
        for row in range(0, width, 16):
            rows = []
            for _ in range(2):
                rows.append(phase)
                phase = phase + first
                first = first + second
            high, low = halves(jnp.concatenate(rows, 0).astype(jnp.float32))
            high_ref[row : row + 16, :] = high
            low_ref[row : row + 16, :] = low

    def multiply(high_ref, low_ref, grads):
        g0, g1 = halves(grads)
        p0, p1 = high_ref[...], low_ref[...]
        total[...] += product(p0, g0) + (product(p0, g1) + product(p1, g0))

    @pl.when(step == 0)
    def _():
        total[...] = jnp.zeros_like(total)
        generate(0, even0, even1)

    start = step * (2 * tile)
    generate(start + tile, odd0, odd1)
    multiply(even0, even1, grads_ref[:, :tile])
    generate(start + 2 * tile, even0, even1)
    multiply(odd0, odd1, grads_ref[:, tile:])

    @pl.when(step == steps - 1)
    def _():
        left, right = total[:, :128], total[:, 128:]
        mine_ref[...] = jnp.where(core == 0, left, right)
        send_ref[...] = jnp.where(core == 0, right, left)


def project(seed, offsets, grads, width):
    queries, coords = grads.shape
    steps = coords // (2 * tile)
    half = jax.ShapeDtypeStruct((width, queries // 2), jnp.float32)
    out_spec = pl.BlockSpec((width, queries // 2), lambda i: (0, 0))
    return pl.pallas_call(
        functools.partial(project_body, width=width, steps=steps),
        grid=(steps,),
        in_specs=[
            pl.BlockSpec(memory_space=pltpu.SMEM),
            pl.BlockSpec(memory_space=pltpu.SMEM),
            pl.BlockSpec((queries, 2 * tile), lambda i: (0, i)),
        ],
        out_specs=[out_spec, out_spec],
        out_shape=[half, half],
        scratch_shapes=[pltpu.VMEM((width, tile), bf16)] * 4 + [pltpu.VMEM((width, queries), jnp.float32)],
        compiler_params=pltpu.CompilerParams(
            dimension_semantics=("arbitrary",),
            vmem_limit_bytes=48 << 20,
        ),
        name="project",
    )(seed, offsets, grads)


def copies_body(parts_ref, copies_ref, *, scale, width, width_total):
    own = parts_ref[0]
    for i in range(1, parts_ref.shape[0]):
        own += parts_ref[i]
    own = own.T
    chip = lax.axis_index("param") // 2
    column = lax.broadcasted_iota(jnp.int32, (1, 128), 1) + (lax.axis_index("proj") * width + chip * 128)
    own = own * (jnp.sqrt(1.0 + 2.0 * column.astype(jnp.float32) / width_total) * (scale * 2.0**-31))
    for i in range(parts_ref.shape[0]):
        copies_ref[i] = own


def whole(shape):
    return pl.BlockSpec(shape, lambda i: (0,) * len(shape))


def summed_copies(parts, param_total, width, width_total):
    peers, rows, cols = parts.shape
    return pl.pallas_call(
        functools.partial(copies_body, scale=math.sqrt(3.0 / param_total), width=width, width_total=width_total),
        grid=(1,),
        in_specs=[whole(parts.shape)],
        out_specs=whole((peers, cols, rows)),
        out_shape=jax.ShapeDtypeStruct((peers, cols, rows), parts.dtype),
        compiler_params=pltpu.CompilerParams(vmem_limit_bytes=8 << 20),
        name="summed_copies",
    )(parts)


def split_body(stored_ref, high_ref, low_ref):
    high_ref[...], low_ref[...] = halves(stored_ref[...])


def split_stored(stored):
    rows, width = stored.shape
    block = pl.BlockSpec((rows // 8, width), lambda i: (i, 0))
    out = jax.ShapeDtypeStruct(stored.shape, bf16)
    return pl.pallas_call(
        split_body,
        grid=(8,),
        in_specs=[block],
        out_specs=[block, block],
        out_shape=[out, out],
        compiler_params=pltpu.CompilerParams(dimension_semantics=("arbitrary",), vmem_limit_bytes=8 << 20),
        name="split_stored",
    )(stored)


def score_body(own_ref, other_ref, high_ref, low_ref, near_ref, far_ref, *, leaving):
    own_half = lax.axis_index("param") % 2
    y = lax.axis_index("proj") // 8
    from_own = own_half == (1 - y if leaving else y)
    highs, lows = [], []
    squares = jnp.zeros((128, 128), jnp.float32)
    for b in range(8):
        value = jnp.where(from_own, own_ref[b], other_ref[b])
        h, l = halves(value)
        highs.append(h)
        lows.append(l)
        squares += value * value
    sums = jnp.broadcast_to(jnp.sum(squares, axis=1, keepdims=True), (128, 128))
    lane = lax.broadcasted_iota(jnp.int32, (8, 128), 1)
    left = jnp.concatenate(highs + lows, 1)
    high = jnp.concatenate(highs, 1)
    for c in range(0, 1024, 256):
        s0, s1 = high_ref[c : c + 256, :], low_ref[c : c + 256, :]
        raw = product(left, jnp.concatenate([s0, s0], 1)) + product(high, s1)
        for z in range(8):
            out_ref = near_ref if z < 4 else far_ref
            for part in range(2):
                row = 16 * (c // 128 + part)
                out_ref[z % 4, row : row + 16, :] = raw[16 * z : 16 * z + 16, 128 * part : 128 * part + 128]
    for z in range(8):
        out_ref = near_ref if z < 4 else far_ref
        out_ref[z % 4, 128:, :] = jnp.where(lane < 64, sums[16 * z : 16 * z + 8], sums[16 * z + 8 : 16 * z + 16])


def scores(own, other, high, low, leaving):
    out = jax.ShapeDtypeStruct((4, 136, 128), jnp.float32)
    return pl.pallas_call(
        functools.partial(score_body, leaving=leaving),
        grid=(1,),
        in_specs=[whole(own.shape), whole(other.shape), whole(high.shape), whole(low.shape)],
        out_specs=[whole(out.shape), whole(out.shape)],
        out_shape=[out, out],
        compiler_params=pltpu.CompilerParams(vmem_limit_bytes=24 << 20),
        name="scores_leaving" if leaving else "scores_kept",
    )(own, other, high, low)


def finish_body(parts_ref, out_ref, *, width_total):
    total = parts_ref[0]
    for i in range(1, 8):
        total += parts_ref[i]
    tail = total[128:]
    sums = jnp.concatenate([tail[:, :1], tail[:, 64:65]], 0)
    factor = lax.rsqrt(sums / width_total + epsilon) * (1.0 / math.sqrt(width_total))
    for c in range(8):
        out_ref[:, 128 * c : 128 * c + 128] = jnp.tanh(total[16 * c : 16 * c + 16] * factor)


def finish(parts, width_total):
    return pl.pallas_call(
        functools.partial(finish_body, width_total=width_total),
        grid=(1,),
        in_specs=[whole(parts.shape)],
        out_specs=whole((16, 1024)),
        out_shape=jax.ShapeDtypeStruct((16, 1024), jnp.float32),
        compiler_params=pltpu.CompilerParams(vmem_limit_bytes=8 << 20),
        name="finish",
    )(parts)


core_swap = [(i, i ^ 1) for i in range(16)]
y_swap = [(i, i ^ 8) for i in range(16)]
chips = [[c + 2 * i for i in range(8)] for c in range(2)]
rings = [[8 * y + z for z in range(8)] for y in range(2)]


def exchanged(x, axis, groups):
    return lax.all_to_all(x, axis, 0, 0, axis_index_groups=groups, tiled=True)


def on_device(query_grads, stored, proj_seed, offsets):
    width = stored.shape[1]
    param_total = query_grads.shape[1] * 16
    width_total = width * 16
    mine, send = project(proj_seed, offsets, query_grads, width)
    high, low = split_stored(stored)
    part = (mine + lax.ppermute(send, "param", core_swap)).reshape(8, width // 8, 128)
    copies = summed_copies(exchanged(part, "param", chips), param_total, width, width_total)
    own = exchanged(copies, "param", chips)
    other = lax.ppermute(own, "param", core_swap)
    leaving = scores(own, other, high, low, True)
    arrived = [lax.ppermute(x, "proj", y_swap) for x in leaving]
    kept = scores(own, other, high, low, False)
    half = jnp.concatenate([a + b for a, b in zip(kept, arrived)])
    return finish(exchanged(half, "proj", rings), width_total)


def solution(mesh):
    placed = (P(None, "param"), P("param", "proj"), P(), P("param"))
    return jax.shard_map(on_device, mesh=mesh, in_specs=placed, out_specs=P("proj", "param"), check_vma=False)
```

```python
import functools
import math

import jax
import jax.numpy as jnp
from jax import lax
from jax.experimental import pallas as pl
from jax.experimental.pallas import tpu as pltpu
from jax.sharding import PartitionSpec as P

modulus = 32749
epsilon = 1e-06
turn_whole = 2**32 // modulus
turn_rest = 2**32 / modulus - turn_whole
tile = 256
NT = (((1,), (1,)), ((), ()))
bf16 = jnp.bfloat16


def reduced(x):
    quotient = (x.astype(jnp.float32) * (1.0 / modulus)).astype(jnp.int32)
    rest = x - quotient * modulus
    rest = jnp.where(rest < 0, rest + modulus, rest)
    return jnp.where(rest >= modulus, rest - modulus, rest)


def turns(residue):
    return residue * turn_whole + jnp.round(residue.astype(jnp.float32) * turn_rest).astype(jnp.int32)


def halves(x):
    high = x.astype(bf16)
    return high, (x - high.astype(jnp.float32)).astype(bf16)


def product(a, b):
    return lax.dot_general(a, b, NT, preferred_element_type=jnp.float32)


def quadratic_start(seed_ref, offset_ref, column_start, coord_start, lanes):
    coord = lax.broadcasted_iota(jnp.int32, (8, lanes), 1) + (coord_start + offset_ref[0])
    column = lax.broadcasted_iota(jnp.int32, (8, lanes), 0) + column_start
    a = reduced(coord * 1103 + seed_ref[0]) + 3
    b = reduced(column * 2111 + seed_ref[1]) + 1
    w = reduced(a * b + 14)
    step = reduced(a * (8 * 2111))
    square = reduced(step * step)
    phase = turns(reduced(w * w + (a - 3))) + (turn_whole // 2 - 2**31)
    first = turns(reduced(2 * reduced(w * step) + square))
    second = turns(reduced(2 * square))
    return phase, first, second


def project_body(seed_ref, offset_ref, grads_ref, mine_ref, send_ref, even0, even1, odd0, odd1, total, *, width, steps):
    step = pl.program_id(0)
    column_start = lax.axis_index("proj") * width
    core = lax.axis_index("param") % 2

    def generate(coord_start, high_ref, low_ref):
        phase, first, second = quadratic_start(seed_ref, offset_ref, column_start, coord_start, tile)
        for row in range(0, width, 16):
            rows = []
            for _ in range(2):
                rows.append(phase)
                phase = phase + first
                first = first + second
            high, low = halves(jnp.concatenate(rows, 0).astype(jnp.float32))
            high_ref[row : row + 16, :] = high
            low_ref[row : row + 16, :] = low

    def multiply(high_ref, low_ref, grads):
        g0, g1 = halves(grads)
        p0, p1 = high_ref[...], low_ref[...]
        total[...] += product(p0, g0) + (product(p0, g1) + product(p1, g0))

    @pl.when(step == 0)
    def _():
        total[...] = jnp.zeros_like(total)
        generate(0, even0, even1)

    start = step * (2 * tile)
    generate(start + tile, odd0, odd1)
    multiply(even0, even1, grads_ref[:, :tile])
    generate(start + 2 * tile, even0, even1)
    multiply(odd0, odd1, grads_ref[:, tile:])

    @pl.when(step == steps - 1)
    def _():
        left, right = total[:, :128], total[:, 128:]
        mine_ref[...] = jnp.where(core == 0, left, right)
        send_ref[...] = jnp.where(core == 0, right, left)


def project(seed, offsets, grads, width):
    queries, coords = grads.shape
    steps = coords // (2 * tile)
    half = jax.ShapeDtypeStruct((width, queries // 2), jnp.float32)
    out_spec = pl.BlockSpec((width, queries // 2), lambda i: (0, 0))
    return pl.pallas_call(
        functools.partial(project_body, width=width, steps=steps),
        grid=(steps,),
        in_specs=[
            pl.BlockSpec(memory_space=pltpu.SMEM),
            pl.BlockSpec(memory_space=pltpu.SMEM),
            pl.BlockSpec((queries, 2 * tile), lambda i: (0, i)),
        ],
        out_specs=[out_spec, out_spec],
        out_shape=[half, half],
        scratch_shapes=[pltpu.VMEM((width, tile), bf16)] * 4 + [pltpu.VMEM((width, queries), jnp.float32)],
        compiler_params=pltpu.CompilerParams(
            dimension_semantics=("arbitrary",),
            vmem_limit_bytes=48 << 20,
        ),
        name="project",
    )(seed, offsets, grads)


def copies_body(parts_ref, copies_ref, *, scale, width, width_total):
    own = parts_ref[0]
    for i in range(1, parts_ref.shape[0]):
        own += parts_ref[i]
    own = own.T
    chip = lax.axis_index("param") // 2
    column = lax.broadcasted_iota(jnp.int32, (1, 128), 1) + (lax.axis_index("proj") * width + chip * 128)
    own = own * (jnp.sqrt(1.0 + 2.0 * column.astype(jnp.float32) / width_total) * (scale * 2.0**-31))
    for i in range(parts_ref.shape[0]):
        copies_ref[i] = own


def whole(shape):
    return pl.BlockSpec(shape, lambda i: (0,) * len(shape))


def summed_copies(parts, param_total, width, width_total):
    peers, rows, cols = parts.shape
    return pl.pallas_call(
        functools.partial(copies_body, scale=math.sqrt(3.0 / param_total), width=width, width_total=width_total),
        grid=(1,),
        in_specs=[whole(parts.shape)],
        out_specs=whole((peers, cols, rows)),
        out_shape=jax.ShapeDtypeStruct((peers, cols, rows), parts.dtype),
        compiler_params=pltpu.CompilerParams(vmem_limit_bytes=8 << 20),
        name="summed_copies",
    )(parts)


def split_body(stored_ref, high_ref, low_ref):
    high_ref[...], low_ref[...] = halves(stored_ref[...])


def split_stored(stored):
    rows, width = stored.shape
    block = pl.BlockSpec((rows // 8, width), lambda i: (i, 0))
    out = jax.ShapeDtypeStruct(stored.shape, bf16)
    return pl.pallas_call(
        split_body,
        grid=(8,),
        in_specs=[block],
        out_specs=[block, block],
        out_shape=[out, out],
        compiler_params=pltpu.CompilerParams(dimension_semantics=("arbitrary",), vmem_limit_bytes=8 << 20),
        name="split_stored",
    )(stored)


def score_body(value_ref, high_ref, low_ref, out_ref):
    highs, lows = [], []
    for b in range(8):
        h, l = halves(value_ref[b])
        highs.append(h)
        lows.append(l)
    left = jnp.concatenate(highs + lows, 1)
    high = jnp.concatenate(highs, 1)
    for c in range(0, 1024, 256):
        s0, s1 = high_ref[c : c + 256, :], low_ref[c : c + 256, :]
        raw = product(left, jnp.concatenate([s0, s0], 1)) + product(high, s1)
        for z in range(8):
            for part in range(2):
                row = 16 * (c // 128 + part)
                out_ref[z, row : row + 16, :] = raw[16 * z : 16 * z + 16, 128 * part : 128 * part + 128]


def scores(value, high, low, name):
    out = jax.ShapeDtypeStruct((8, 128, 128), jnp.float32)
    return pl.pallas_call(
        score_body,
        grid=(1,),
        in_specs=[whole(value.shape), whole(high.shape), whole(low.shape)],
        out_specs=whole(out.shape),
        out_shape=out,
        compiler_params=pltpu.CompilerParams(vmem_limit_bytes=24 << 20),
        name=name,
    )(value, high, low)


def square_body(own_ref, other_ref, out_ref):
    sums = []
    for value_ref in (own_ref, other_ref):
        squares = jnp.zeros((128, 128), jnp.float32)
        for b in range(8):
            squares += value_ref[b] * value_ref[b]
        sums.append(jnp.broadcast_to(jnp.sum(squares, axis=1, keepdims=True), (128, 128)).T[:8])
    row = lax.broadcasted_iota(jnp.int32, (8, 128), 0)
    out_ref[...] = jnp.where(row == lax.axis_index("param") % 2, sums[0], sums[1])


def square_sums(own, other):
    return pl.pallas_call(
        square_body,
        grid=(1,),
        in_specs=[whole(own.shape), whole(other.shape)],
        out_specs=whole((8, 128)),
        out_shape=jax.ShapeDtypeStruct((8, 128), jnp.float32),
        compiler_params=pltpu.CompilerParams(vmem_limit_bytes=8 << 20),
        name="square_sums",
    )(own, other)


def join_body(own_ref, other_ref, first_ref, second_ref, sums_ref, out_ref, passed_ref):
    stays = lax.axis_index("param") % 2 == lax.axis_index("proj") // 8
    for z in range(8):
        out_ref[z] = jnp.where(stays, own_ref[z] + first_ref[z], other_ref[z] + second_ref[z])
    passed_ref[...] = sums_ref[...]


def joined(own, other, first, second, sums):
    return pl.pallas_call(
        join_body,
        grid=(1,),
        in_specs=[whole(own.shape)] * 4 + [whole(sums.shape)],
        out_specs=[whole(own.shape), whole(sums.shape)],
        out_shape=[jax.ShapeDtypeStruct(own.shape, own.dtype), jax.ShapeDtypeStruct(sums.shape, sums.dtype)],
        compiler_params=pltpu.CompilerParams(vmem_limit_bytes=16 << 20),
        name="joined",
    )(own, other, first, second, sums)


def finish_body(parts_ref, sums_ref, out_ref, *, width_total):
    total = parts_ref[0]
    for i in range(1, 8):
        total += parts_ref[i]
    place = lax.axis_index("proj")
    sums = jnp.where(place < 8, sums_ref[:1], sums_ref[1:2])
    row = lax.broadcasted_iota(jnp.int32, (16, 128), 0) + 16 * (place % 8)
    chosen = jnp.where(row == lax.broadcasted_iota(jnp.int32, (16, 128), 1), sums, 0.0)
    column = jnp.sum(chosen, axis=1, keepdims=True)
    factor = lax.rsqrt(column / width_total + epsilon) * (1.0 / math.sqrt(width_total))
    for c in range(8):
        out_ref[:, 128 * c : 128 * c + 128] = jnp.tanh(total[16 * c : 16 * c + 16] * factor)


def finish(parts, sums, width_total):
    return pl.pallas_call(
        functools.partial(finish_body, width_total=width_total),
        grid=(1,),
        in_specs=[whole(parts.shape), whole(sums.shape)],
        out_specs=whole((16, 1024)),
        out_shape=jax.ShapeDtypeStruct((16, 1024), jnp.float32),
        compiler_params=pltpu.CompilerParams(vmem_limit_bytes=8 << 20),
        name="finish",
    )(parts, sums)


core_swap = [(i, i ^ 1) for i in range(16)]
leaving = [
    [(16 * p + 8 * y + z, 16 * p + 8 * (1 - y) + z) for p in range(16) for y in range(2) for z in range(8) if (p % 2 == y) == second]
    for second in (False, True)
]
chips = [[c + 2 * i for i in range(8)] for c in range(2)]
rings = [[8 * y + z for z in range(8)] for y in range(2)]


def exchanged(x, axis, groups):
    return lax.all_to_all(x, axis, 0, 0, axis_index_groups=groups, tiled=True)


def on_device(query_grads, stored, proj_seed, offsets):
    width = stored.shape[1]
    param_total = query_grads.shape[1] * 16
    width_total = width * 16
    mine, send = project(proj_seed, offsets, query_grads, width)
    high, low = split_stored(stored)
    part = (mine + lax.ppermute(send, "param", core_swap)).reshape(8, width // 8, 128)
    copies = summed_copies(exchanged(part, "param", chips), param_total, width, width_total)
    own = exchanged(copies, "param", chips)
    other = lax.ppermute(own, "param", core_swap)
    sums = square_sums(own, other)
    own_scores = scores(own, high, low, "scores_own")
    first = lax.ppermute(own_scores, ("param", "proj"), leaving[0])
    other_scores = scores(other, high, low, "scores_other")
    second = lax.ppermute(other_scores, ("param", "proj"), leaving[1])
    for peers in ((8, 1, 9), (2, 4, 6)):
        sums = sum([lax.ppermute(sums, "proj", [(i, i ^ peer) for i in range(16)]) for peer in peers], sums)
    half, sums = joined(own_scores, other_scores, first, second, sums)
    return finish(exchanged(half, "proj", rings), sums, width_total)


def solution(mesh):
    placed = (P(None, "param"), P("param", "proj"), P(), P("param"))
    return jax.shard_map(on_device, mesh=mesh, in_specs=placed, out_specs=P("proj", "param"), check_vma=False)
```

```python
import functools
import math

import jax
import jax.numpy as jnp
from jax import lax
from jax.experimental import pallas as pl
from jax.experimental.pallas import tpu as pltpu
from jax.sharding import PartitionSpec as P

modulus = 32749
epsilon = 1e-06
turn_whole = 2**32 // modulus
turn_rest = 2**32 / modulus - turn_whole
tile = 512
NT = (((1,), (1,)), ((), ()))
bf16 = jnp.bfloat16


def reduced(x):
    quotient = (x.astype(jnp.float32) * (1.0 / modulus)).astype(jnp.int32)
    rest = x - quotient * modulus
    rest = jnp.where(rest < 0, rest + modulus, rest)
    return jnp.where(rest >= modulus, rest - modulus, rest)


def turns(residue):
    return residue * turn_whole + jnp.round(residue.astype(jnp.float32) * turn_rest).astype(jnp.int32)


def halves(x):
    high = x.astype(bf16)
    return high, (x - high.astype(jnp.float32)).astype(bf16)


def product(a, b):
    return lax.dot_general(a, b, NT, preferred_element_type=jnp.float32)


def quadratic_start(seed_ref, offset_ref, column_start, coord_start, lanes):
    coord = lax.broadcasted_iota(jnp.int32, (8, lanes), 1) + (coord_start + offset_ref[0])
    column = lax.broadcasted_iota(jnp.int32, (8, lanes), 0) + column_start
    a = reduced(coord * 1103 + seed_ref[0]) + 3
    b = reduced(column * 2111 + seed_ref[1]) + 1
    w = reduced(a * b + 14)
    step = reduced(a * (8 * 2111))
    square = reduced(step * step)
    phase = turns(reduced(w * w + (a - 3))) + (turn_whole // 2 - 2**31)
    first = turns(reduced(2 * reduced(w * step) + square))
    second = turns(reduced(2 * square))
    return phase, first, second


def project_body(seed_ref, offset_ref, grads_ref, mine_ref, send_ref, even0, even1, odd0, odd1, total, *, width, steps):
    step = pl.program_id(0)
    column_start = lax.axis_index("proj") * width
    core = lax.axis_index("param") % 2

    def generate(coord_start, high_ref, low_ref):
        phase, first, second = quadratic_start(seed_ref, offset_ref, column_start, coord_start, tile)
        for row in range(0, width, 16):
            rows = []
            for _ in range(2):
                rows.append(phase)
                phase = phase + first
                first = first + second
            high, low = halves(jnp.concatenate(rows, 0).astype(jnp.float32))
            high_ref[row : row + 16, :] = high
            low_ref[row : row + 16, :] = low

    def multiply(high_ref, low_ref, grads):
        g0, g1 = halves(grads)
        p0, p1 = high_ref[...], low_ref[...]
        total[...] += product(p0, g0) + (product(p0, g1) + product(p1, g0))

    @pl.when(step == 0)
    def _():
        total[...] = jnp.zeros_like(total)
        generate(0, even0, even1)

    start = step * (2 * tile)
    generate(start + tile, odd0, odd1)
    multiply(even0, even1, grads_ref[:, :tile])
    generate(start + 2 * tile, even0, even1)
    multiply(odd0, odd1, grads_ref[:, tile:])

    @pl.when(step == steps - 1)
    def _():
        left, right = total[:, :128], total[:, 128:]
        mine_ref[...] = jnp.where(core == 0, left, right)
        send_ref[...] = jnp.where(core == 0, right, left)


def project(seed, offsets, grads, width):
    queries, coords = grads.shape
    steps = coords // (2 * tile)
    half = jax.ShapeDtypeStruct((width, queries // 2), jnp.float32)
    out_spec = pl.BlockSpec((width, queries // 2), lambda i: (0, 0))
    return pl.pallas_call(
        functools.partial(project_body, width=width, steps=steps),
        grid=(steps,),
        in_specs=[
            pl.BlockSpec(memory_space=pltpu.SMEM),
            pl.BlockSpec(memory_space=pltpu.SMEM),
            pl.BlockSpec((queries, 2 * tile), lambda i: (0, i)),
        ],
        out_specs=[out_spec, out_spec],
        out_shape=[half, half],
        scratch_shapes=[pltpu.VMEM((width, tile), bf16)] * 4 + [pltpu.VMEM((width, queries), jnp.float32)],
        compiler_params=pltpu.CompilerParams(
            dimension_semantics=("arbitrary",),
            vmem_limit_bytes=48 << 20,
        ),
        name="project",
    )(seed, offsets, grads)


def copies_body(parts_ref, copies_ref, *, scale, width, width_total):
    own = parts_ref[0]
    for i in range(1, parts_ref.shape[0]):
        own += parts_ref[i]
    own = own.T
    chip = lax.axis_index("param") // 2
    column = lax.broadcasted_iota(jnp.int32, (1, 128), 1) + (lax.axis_index("proj") * width + chip * 128)
    own = own * (jnp.sqrt(1.0 + 2.0 * column.astype(jnp.float32) / width_total) * (scale * 2.0**-31))
    for i in range(parts_ref.shape[0]):
        copies_ref[i] = own


def whole(shape):
    return pl.BlockSpec(shape, lambda i: (0,) * len(shape))


def summed_copies(parts, param_total, width, width_total):
    peers, rows, cols = parts.shape
    return pl.pallas_call(
        functools.partial(copies_body, scale=math.sqrt(3.0 / param_total), width=width, width_total=width_total),
        grid=(1,),
        in_specs=[whole(parts.shape)],
        out_specs=whole((peers, cols, rows)),
        out_shape=jax.ShapeDtypeStruct((peers, cols, rows), parts.dtype),
        compiler_params=pltpu.CompilerParams(vmem_limit_bytes=8 << 20),
        name="summed_copies",
    )(parts)


def split_body(stored_ref, high_ref, low_ref):
    high_ref[...], low_ref[...] = halves(stored_ref[...])


def split_stored(stored):
    rows, width = stored.shape
    block = pl.BlockSpec((rows // 8, width), lambda i: (i, 0))
    out = jax.ShapeDtypeStruct(stored.shape, bf16)
    return pl.pallas_call(
        split_body,
        grid=(8,),
        in_specs=[block],
        out_specs=[block, block],
        out_shape=[out, out],
        compiler_params=pltpu.CompilerParams(dimension_semantics=("arbitrary",), vmem_limit_bytes=8 << 20),
        name="split_stored",
    )(stored)


def score_body(value_ref, high_ref, low_ref, out_ref):
    highs, lows = [], []
    squares = jnp.zeros((128, 128), jnp.float32)
    for b in range(8):
        value = value_ref[b]
        h, l = halves(value)
        highs.append(h)
        lows.append(l)
        squares += value * value
    sums = jnp.broadcast_to(jnp.sum(squares, axis=1, keepdims=True), (128, 128))
    lane = lax.broadcasted_iota(jnp.int32, (8, 128), 1)
    left = jnp.concatenate(highs + lows, 1)
    high = jnp.concatenate(highs, 1)
    for c in range(0, 1024, 256):
        s0, s1 = high_ref[c : c + 256, :], low_ref[c : c + 256, :]
        raw = product(left, jnp.concatenate([s0, s0], 1)) + product(high, s1)
        for z in range(8):
            for part in range(2):
                row = 16 * (c // 128 + part)
                out_ref[z, row : row + 16, :] = raw[16 * z : 16 * z + 16, 128 * part : 128 * part + 128]
    for z in range(8):
        out_ref[z, 128:, :] = jnp.where(lane < 64, sums[16 * z : 16 * z + 8], sums[16 * z + 8 : 16 * z + 16])


def scores(value, high, low, name):
    out = jax.ShapeDtypeStruct((8, 136, 128), jnp.float32)
    return pl.pallas_call(
        score_body,
        grid=(1,),
        in_specs=[whole(value.shape), whole(high.shape), whole(low.shape)],
        out_specs=whole(out.shape),
        out_shape=out,
        compiler_params=pltpu.CompilerParams(vmem_limit_bytes=24 << 20),
        name=name,
    )(value, high, low)


def join_body(own_ref, other_ref, first_ref, second_ref, out_ref):
    stays = lax.axis_index("param") % 2 == lax.axis_index("proj") // 8
    for z in range(8):
        out_ref[z] = jnp.where(stays, own_ref[z] + first_ref[z], other_ref[z] + second_ref[z])


def joined(own, other, first, second):
    return pl.pallas_call(
        join_body,
        grid=(1,),
        in_specs=[whole(own.shape)] * 4,
        out_specs=whole(own.shape),
        out_shape=jax.ShapeDtypeStruct(own.shape, own.dtype),
        compiler_params=pltpu.CompilerParams(vmem_limit_bytes=16 << 20),
        name="joined",
    )(own, other, first, second)


def finish_body(parts_ref, out_ref, *, width_total):
    total = parts_ref[0]
    for i in range(1, 8):
        total += parts_ref[i]
    tail = total[128:]
    sums = jnp.concatenate([tail[:, :1], tail[:, 64:65]], 0)
    factor = lax.rsqrt(sums / width_total + epsilon) * (1.0 / math.sqrt(width_total))
    for c in range(8):
        out_ref[:, 128 * c : 128 * c + 128] = jnp.tanh(total[16 * c : 16 * c + 16] * factor)


def finish(parts, width_total):
    return pl.pallas_call(
        functools.partial(finish_body, width_total=width_total),
        grid=(1,),
        in_specs=[whole(parts.shape)],
        out_specs=whole((16, 1024)),
        out_shape=jax.ShapeDtypeStruct((16, 1024), jnp.float32),
        compiler_params=pltpu.CompilerParams(vmem_limit_bytes=8 << 20),
        name="finish",
    )(parts)


core_swap = [(i, i ^ 1) for i in range(16)]
leaving = [
    [(16 * p + 8 * y + z, 16 * p + 8 * (1 - y) + z) for p in range(16) for y in range(2) for z in range(8) if (p % 2 == y) == second]
    for second in (False, True)
]
chips = [[c + 2 * i for i in range(8)] for c in range(2)]
rings = [[8 * y + z for z in range(8)] for y in range(2)]


def exchanged(x, axis, groups):
    return lax.all_to_all(x, axis, 0, 0, axis_index_groups=groups, tiled=True)


def on_device(query_grads, stored, proj_seed, offsets):
    width = stored.shape[1]
    param_total = query_grads.shape[1] * 16
    width_total = width * 16
    mine, send = project(proj_seed, offsets, query_grads, width)
    high, low = split_stored(stored)
    part = (mine + lax.ppermute(send, "param", core_swap)).reshape(8, width // 8, 128)
    copies = summed_copies(exchanged(part, "param", chips), param_total, width, width_total)
    own = exchanged(copies, "param", chips)
    other = lax.ppermute(own, "param", core_swap)
    own_scores = scores(own, high, low, "scores_own")
    first = lax.ppermute(own_scores, ("param", "proj"), leaving[0])
    other_scores = scores(other, high, low, "scores_other")
    second = lax.ppermute(other_scores, ("param", "proj"), leaving[1])
    half = joined(own_scores, other_scores, first, second)
    return finish(exchanged(half, "proj", rings), width_total)


def solution(mesh):
    placed = (P(None, "param"), P("param", "proj"), P(), P("param"))
    return jax.shard_map(on_device, mesh=mesh, in_specs=placed, out_specs=P("proj", "param"), check_vma=False)
```

```python
import functools
import math

import jax
import jax.numpy as jnp
from jax import lax
from jax.experimental import pallas as pl
from jax.experimental.pallas import tpu as pltpu
from jax.sharding import PartitionSpec as P

modulus = 32749
epsilon = 1e-06
turn_whole = 2**32 // modulus
turn_rest = 2**32 / modulus - turn_whole
tile = 512
NT = (((1,), (1,)), ((), ()))
bf16 = jnp.bfloat16


def reduced(x):
    quotient = (x.astype(jnp.float32) * (1.0 / modulus)).astype(jnp.int32)
    rest = x - quotient * modulus
    rest = jnp.where(rest < 0, rest + modulus, rest)
    return jnp.where(rest >= modulus, rest - modulus, rest)


def turns(residue):
    return residue * turn_whole + jnp.round(residue.astype(jnp.float32) * turn_rest).astype(jnp.int32)


def halves(x):
    high = x.astype(bf16)
    return high, (x - high.astype(jnp.float32)).astype(bf16)


def product(a, b):
    return lax.dot_general(a, b, NT, preferred_element_type=jnp.float32)


def quadratic_start(seed_ref, offset_ref, column_start, coord_start, lanes):
    coord = lax.broadcasted_iota(jnp.int32, (8, lanes), 1) + (coord_start + offset_ref[0])
    column = lax.broadcasted_iota(jnp.int32, (8, lanes), 0) + column_start
    a = reduced(coord * 1103 + seed_ref[0]) + 3
    b = reduced(column * 2111 + seed_ref[1]) + 1
    w = reduced(a * b + 14)
    step = reduced(a * (8 * 2111))
    square = reduced(step * step)
    phase = turns(reduced(w * w + (a - 3))) + (turn_whole // 2 - 2**31)
    first = turns(reduced(2 * reduced(w * step) + square))
    second = turns(reduced(2 * square))
    return phase, first, second


def project_body(seed_ref, offset_ref, grads_ref, mine_ref, send_ref, even0, even1, odd0, odd1, total, *, width, steps):
    step = pl.program_id(0)
    column_start = lax.axis_index("proj") * width
    core = lax.axis_index("param") % 2

    def generate(coord_start, high_ref, low_ref):
        phase, first, second = quadratic_start(seed_ref, offset_ref, column_start, coord_start, tile)
        for row in range(0, width, 16):
            rows = []
            for _ in range(2):
                rows.append(phase)
                phase = phase + first
                first = first + second
            high, low = halves(jnp.concatenate(rows, 0).astype(jnp.float32))
            high_ref[row : row + 16, :] = high
            low_ref[row : row + 16, :] = low

    def multiply(high_ref, low_ref, grads):
        g0, g1 = halves(grads)
        p0, p1 = high_ref[...], low_ref[...]
        total[...] += product(p0, g0) + (product(p0, g1) + product(p1, g0))

    @pl.when(step == 0)
    def _():
        total[...] = jnp.zeros_like(total)
        generate(0, even0, even1)

    start = step * (2 * tile)
    generate(start + tile, odd0, odd1)
    multiply(even0, even1, grads_ref[:, :tile])
    generate(start + 2 * tile, even0, even1)
    multiply(odd0, odd1, grads_ref[:, tile:])

    @pl.when(step == steps - 1)
    def _():
        left, right = total[:, :128], total[:, 128:]
        mine_ref[...] = jnp.where(core == 0, left, right)
        send_ref[...] = jnp.where(core == 0, right, left)


def project(seed, offsets, grads, width):
    queries, coords = grads.shape
    steps = coords // (2 * tile)
    half = jax.ShapeDtypeStruct((width, queries // 2), jnp.float32)
    out_spec = pl.BlockSpec((width, queries // 2), lambda i: (0, 0))
    return pl.pallas_call(
        functools.partial(project_body, width=width, steps=steps),
        grid=(steps,),
        in_specs=[
            pl.BlockSpec(memory_space=pltpu.SMEM),
            pl.BlockSpec(memory_space=pltpu.SMEM),
            pl.BlockSpec((queries, 2 * tile), lambda i: (0, i)),
        ],
        out_specs=[out_spec, out_spec],
        out_shape=[half, half],
        scratch_shapes=[pltpu.VMEM((width, tile), bf16)] * 4 + [pltpu.VMEM((width, queries), jnp.float32)],
        compiler_params=pltpu.CompilerParams(
            dimension_semantics=("arbitrary",),
            vmem_limit_bytes=48 << 20,
        ),
        name="project",
    )(seed, offsets, grads)


def copies_body(parts_ref, copies_ref, *, scale, width, width_total):
    own = parts_ref[0]
    for i in range(1, parts_ref.shape[0]):
        own += parts_ref[i]
    own = own.T
    chip = lax.axis_index("param") // 2
    column = lax.broadcasted_iota(jnp.int32, (1, 128), 1) + (lax.axis_index("proj") * width + chip * 128)
    own = own * (jnp.sqrt(1.0 + 2.0 * column.astype(jnp.float32) / width_total) * (scale * 2.0**-31))
    for i in range(parts_ref.shape[0]):
        copies_ref[i] = own


def whole(shape):
    return pl.BlockSpec(shape, lambda i: (0,) * len(shape))


def summed_copies(parts, param_total, width, width_total):
    peers, rows, cols = parts.shape
    return pl.pallas_call(
        functools.partial(copies_body, scale=math.sqrt(3.0 / param_total), width=width, width_total=width_total),
        grid=(1,),
        in_specs=[whole(parts.shape)],
        out_specs=whole((peers, cols, rows)),
        out_shape=jax.ShapeDtypeStruct((peers, cols, rows), parts.dtype),
        compiler_params=pltpu.CompilerParams(vmem_limit_bytes=8 << 20),
        name="summed_copies",
    )(parts)


def split_body(stored_ref, high_ref, low_ref):
    high_ref[...], low_ref[...] = halves(stored_ref[...])


def split_stored(stored):
    rows, width = stored.shape
    block = pl.BlockSpec((rows // 8, width), lambda i: (i, 0))
    out = jax.ShapeDtypeStruct(stored.shape, bf16)
    return pl.pallas_call(
        split_body,
        grid=(8,),
        in_specs=[block],
        out_specs=[block, block],
        out_shape=[out, out],
        compiler_params=pltpu.CompilerParams(dimension_semantics=("arbitrary",), vmem_limit_bytes=8 << 20),
        name="split_stored",
    )(stored)


def score_body(own_ref, other_ref, high_ref, low_ref, near_ref, far_ref, *, leaving):
    own_half = lax.axis_index("param") % 2
    y = lax.axis_index("proj") // 8
    from_own = own_half == (1 - y if leaving else y)
    highs, lows = [], []
    squares = jnp.zeros((128, 128), jnp.float32)
    for b in range(8):
        value = jnp.where(from_own, own_ref[b], other_ref[b])
        h, l = halves(value)
        highs.append(h)
        lows.append(l)
        squares += value * value
    sums = jnp.broadcast_to(jnp.sum(squares, axis=1, keepdims=True), (128, 128))
    lane = lax.broadcasted_iota(jnp.int32, (8, 128), 1)
    left = jnp.concatenate(highs + lows, 1)
    high = jnp.concatenate(highs, 1)
    for c in range(0, 1024, 256):
        s0, s1 = high_ref[c : c + 256, :], low_ref[c : c + 256, :]
        raw = product(left, jnp.concatenate([s0, s0], 1)) + product(high, s1)
        for z in range(8):
            out_ref = near_ref if z < 4 else far_ref
            for part in range(2):
                row = 16 * (c // 128 + part)
                out_ref[z % 4, row : row + 16, :] = raw[16 * z : 16 * z + 16, 128 * part : 128 * part + 128]
    for z in range(8):
        out_ref = near_ref if z < 4 else far_ref
        out_ref[z % 4, 128:, :] = jnp.where(lane < 64, sums[16 * z : 16 * z + 8], sums[16 * z + 8 : 16 * z + 16])


def scores(own, other, high, low, leaving):
    out = jax.ShapeDtypeStruct((4, 136, 128), jnp.float32)
    return pl.pallas_call(
        functools.partial(score_body, leaving=leaving),
        grid=(1,),
        in_specs=[whole(own.shape), whole(other.shape), whole(high.shape), whole(low.shape)],
        out_specs=[whole(out.shape), whole(out.shape)],
        out_shape=[out, out],
        compiler_params=pltpu.CompilerParams(vmem_limit_bytes=24 << 20),
        name="scores_leaving" if leaving else "scores_kept",
    )(own, other, high, low)


def finish_body(parts_ref, out_ref, *, width_total):
    total = parts_ref[0]
    for i in range(1, 8):
        total += parts_ref[i]
    tail = total[128:]
    sums = jnp.concatenate([tail[:, :1], tail[:, 64:65]], 0)
    factor = lax.rsqrt(sums / width_total + epsilon) * (1.0 / math.sqrt(width_total))
    for c in range(8):
        out_ref[:, 128 * c : 128 * c + 128] = jnp.tanh(total[16 * c : 16 * c + 16] * factor)


def finish(parts, width_total):
    return pl.pallas_call(
        functools.partial(finish_body, width_total=width_total),
        grid=(1,),
        in_specs=[whole(parts.shape)],
        out_specs=whole((16, 1024)),
        out_shape=jax.ShapeDtypeStruct((16, 1024), jnp.float32),
        compiler_params=pltpu.CompilerParams(vmem_limit_bytes=8 << 20),
        name="finish",
    )(parts)


core_swap = [(i, i ^ 1) for i in range(16)]
y_swap = [(i, i ^ 8) for i in range(16)]
chips = [[c + 2 * i for i in range(8)] for c in range(2)]
rings = [[8 * y + z for z in range(8)] for y in range(2)]


def exchanged(x, axis, groups):
    return lax.all_to_all(x, axis, 0, 0, axis_index_groups=groups, tiled=True)


def on_device(query_grads, stored, proj_seed, offsets):
    width = stored.shape[1]
    param_total = query_grads.shape[1] * 16
    width_total = width * 16
    mine, send = project(proj_seed, offsets, query_grads, width)
    high, low = split_stored(stored)
    part = (mine + lax.ppermute(send, "param", core_swap)).reshape(8, width // 8, 128)
    copies = summed_copies(exchanged(part, "param", chips), param_total, width, width_total)
    own = exchanged(copies, "param", chips)
    other = lax.ppermute(own, "param", core_swap)
    leaving = scores(own, other, high, low, True)
    arrived = [lax.ppermute(x, "proj", y_swap) for x in leaving]
    kept = scores(own, other, high, low, False)
    half = jnp.concatenate([a + b for a, b in zip(kept, arrived)])
    return finish(exchanged(half, "proj", rings), width_total)


def solution(mesh):
    placed = (P(None, "param"), P("param", "proj"), P(), P("param"))
    return jax.shard_map(on_device, mesh=mesh, in_specs=placed, out_specs=P("proj", "param"), check_vma=False)
```

```python
import functools
import math

import jax
import jax.numpy as jnp
from jax import lax
from jax.experimental import pallas as pl
from jax.experimental.pallas import tpu as pltpu
from jax.sharding import PartitionSpec as P

modulus = 32749
epsilon = 1e-06
turn_whole = 2**32 // modulus
turn_rest = 2**32 / modulus - turn_whole
tile = 512
NT = (((1,), (1,)), ((), ()))
bf16 = jnp.bfloat16


def reduced(x):
    quotient = (x.astype(jnp.float32) * (1.0 / modulus)).astype(jnp.int32)
    rest = x - quotient * modulus
    rest = jnp.where(rest < 0, rest + modulus, rest)
    return jnp.where(rest >= modulus, rest - modulus, rest)


def turns(residue):
    return residue * turn_whole + jnp.round(residue.astype(jnp.float32) * turn_rest).astype(jnp.int32)


def halves(x):
    high = x.astype(bf16)
    return high, (x - high.astype(jnp.float32)).astype(bf16)


def product(a, b):
    return lax.dot_general(a, b, NT, preferred_element_type=jnp.float32)


def quadratic_start(seed_ref, offset_ref, column_start, coord_start, lanes):
    coord = lax.broadcasted_iota(jnp.int32, (8, lanes), 1) + (coord_start + offset_ref[0])
    column = lax.broadcasted_iota(jnp.int32, (8, lanes), 0) + column_start
    a = reduced(coord * 1103 + seed_ref[0]) + 3
    b = reduced(column * 2111 + seed_ref[1]) + 1
    w = reduced(a * b + 14)
    step = reduced(a * (8 * 2111))
    square = reduced(step * step)
    phase = turns(reduced(w * w + (a - 3))) + (turn_whole // 2 - 2**31)
    first = turns(reduced(2 * reduced(w * step) + square))
    second = turns(reduced(2 * square))
    return phase, first, second


def project_body(seed_ref, offset_ref, grads_ref, mine_ref, send_ref, even0, even1, odd0, odd1, total, *, width, steps):
    step = pl.program_id(0)
    column_start = lax.axis_index("proj") * width
    core = lax.axis_index("param") % 2

    def generate(coord_start, high_ref, low_ref):
        phase, first, second = quadratic_start(seed_ref, offset_ref, column_start, coord_start, tile)
        for row in range(0, width, 16):
            rows = []
            for _ in range(2):
                rows.append(phase)
                phase = phase + first
                first = first + second
            high, low = halves(jnp.concatenate(rows, 0).astype(jnp.float32))
            high_ref[row : row + 16, :] = high
            low_ref[row : row + 16, :] = low

    def multiply(high_ref, low_ref, grads):
        g0, g1 = halves(grads)
        p0, p1 = high_ref[...], low_ref[...]
        total[...] += product(p0, g0) + (product(p0, g1) + product(p1, g0))

    @pl.when(step == 0)
    def _():
        total[...] = jnp.zeros_like(total)
        generate(0, even0, even1)

    start = step * (2 * tile)
    generate(start + tile, odd0, odd1)
    multiply(even0, even1, grads_ref[:, :tile])
    generate(start + 2 * tile, even0, even1)
    multiply(odd0, odd1, grads_ref[:, tile:])

    @pl.when(step == steps - 1)
    def _():
        left, right = total[:, :128], total[:, 128:]
        mine_ref[...] = jnp.where(core == 0, left, right)
        send_ref[...] = jnp.where(core == 0, right, left)


def project(seed, offsets, grads, width):
    queries, coords = grads.shape
    steps = coords // (2 * tile)
    half = jax.ShapeDtypeStruct((width, queries // 2), jnp.float32)
    out_spec = pl.BlockSpec((width, queries // 2), lambda i: (0, 0))
    return pl.pallas_call(
        functools.partial(project_body, width=width, steps=steps),
        grid=(steps,),
        in_specs=[
            pl.BlockSpec(memory_space=pltpu.SMEM),
            pl.BlockSpec(memory_space=pltpu.SMEM),
            pl.BlockSpec((queries, 2 * tile), lambda i: (0, i)),
        ],
        out_specs=[out_spec, out_spec],
        out_shape=[half, half],
        scratch_shapes=[pltpu.VMEM((width, tile), bf16)] * 4 + [pltpu.VMEM((width, queries), jnp.float32)],
        compiler_params=pltpu.CompilerParams(
            dimension_semantics=("arbitrary",),
            vmem_limit_bytes=48 << 20,
        ),
        name="project",
    )(seed, offsets, grads)


def copies_body(parts_ref, copies_ref, *, scale, width, width_total):
    own = parts_ref[0]
    for i in range(1, parts_ref.shape[0]):
        own += parts_ref[i]
    own = own.T
    chip = lax.axis_index("param") // 2
    column = lax.broadcasted_iota(jnp.int32, (1, 128), 1) + (lax.axis_index("proj") * width + chip * 128)
    own = own * (jnp.sqrt(1.0 + 2.0 * column.astype(jnp.float32) / width_total) * (scale * 2.0**-31))
    for i in range(parts_ref.shape[0]):
        copies_ref[i] = own


def whole(shape):
    return pl.BlockSpec(shape, lambda i: (0,) * len(shape))


def summed_copies(parts, param_total, width, width_total):
    peers, rows, cols = parts.shape
    return pl.pallas_call(
        functools.partial(copies_body, scale=math.sqrt(3.0 / param_total), width=width, width_total=width_total),
        grid=(1,),
        in_specs=[whole(parts.shape)],
        out_specs=whole((peers, cols, rows)),
        out_shape=jax.ShapeDtypeStruct((peers, cols, rows), parts.dtype),
        compiler_params=pltpu.CompilerParams(vmem_limit_bytes=8 << 20),
        name="summed_copies",
    )(parts)


def split_body(stored_ref, high_ref, low_ref):
    high_ref[...], low_ref[...] = halves(stored_ref[...])


def split_stored(stored):
    rows, width = stored.shape
    block = pl.BlockSpec((rows // 8, width), lambda i: (i, 0))
    out = jax.ShapeDtypeStruct(stored.shape, bf16)
    return pl.pallas_call(
        split_body,
        grid=(8,),
        in_specs=[block],
        out_specs=[block, block],
        out_shape=[out, out],
        compiler_params=pltpu.CompilerParams(dimension_semantics=("arbitrary",), vmem_limit_bytes=8 << 20),
        name="split_stored",
    )(stored)


def score_body(own_ref, other_ref, high_ref, low_ref, *out_refs, leaving):
    own_half = lax.axis_index("param") % 2
    y = lax.axis_index("proj") // 8
    from_own = own_half == (1 - y if leaving else y)
    highs, lows = [], []
    squares = jnp.zeros((128, 128), jnp.float32)
    for b in range(8):
        value = jnp.where(from_own, own_ref[b], other_ref[b])
        h, l = halves(value)
        highs.append(h)
        lows.append(l)
        squares += value * value
    sums = jnp.broadcast_to(jnp.sum(squares, axis=1, keepdims=True), (128, 128))
    lane = lax.broadcasted_iota(jnp.int32, (8, 128), 1)
    left = jnp.concatenate(highs + lows, 1)
    high = jnp.concatenate(highs, 1)
    for c in range(0, 1024, 256):
        s0, s1 = high_ref[c : c + 256, :], low_ref[c : c + 256, :]
        raw = product(left, jnp.concatenate([s0, s0], 1)) + product(high, s1)
        for z in range(8):
            for part in range(2):
                row = 16 * (c // 128 + part)
                out_refs[z // 2][z % 2, row : row + 16, :] = raw[16 * z : 16 * z + 16, 128 * part : 128 * part + 128]
    for z in range(8):
        out_refs[z // 2][z % 2, 128:, :] = jnp.where(lane < 64, sums[16 * z : 16 * z + 8], sums[16 * z + 8 : 16 * z + 16])


def scores(own, other, high, low, leaving):
    out = jax.ShapeDtypeStruct((2, 136, 128), jnp.float32)
    return pl.pallas_call(
        functools.partial(score_body, leaving=leaving),
        grid=(1,),
        in_specs=[whole(own.shape), whole(other.shape), whole(high.shape), whole(low.shape)],
        out_specs=[whole(out.shape)] * 4,
        out_shape=[out] * 4,
        compiler_params=pltpu.CompilerParams(vmem_limit_bytes=24 << 20),
        name="scores_leaving" if leaving else "scores_kept",
    )(own, other, high, low)


def finish_body(parts_ref, out_ref, *, width_total):
    total = parts_ref[0]
    for i in range(1, 8):
        total += parts_ref[i]
    tail = total[128:]
    sums = jnp.concatenate([tail[:, :1], tail[:, 64:65]], 0)
    factor = lax.rsqrt(sums / width_total + epsilon) * (1.0 / math.sqrt(width_total))
    for c in range(8):
        out_ref[:, 128 * c : 128 * c + 128] = jnp.tanh(total[16 * c : 16 * c + 16] * factor)


def finish(parts, width_total):
    return pl.pallas_call(
        functools.partial(finish_body, width_total=width_total),
        grid=(1,),
        in_specs=[whole(parts.shape)],
        out_specs=whole((16, 1024)),
        out_shape=jax.ShapeDtypeStruct((16, 1024), jnp.float32),
        compiler_params=pltpu.CompilerParams(vmem_limit_bytes=8 << 20),
        name="finish",
    )(parts)


core_swap = [(i, i ^ 1) for i in range(16)]
y_swap = [(i, i ^ 8) for i in range(16)]
chips = [[c + 2 * i for i in range(8)] for c in range(2)]
rings = [[8 * y + z for z in range(8)] for y in range(2)]


def exchanged(x, axis, groups):
    return lax.all_to_all(x, axis, 0, 0, axis_index_groups=groups, tiled=True)


def on_device(query_grads, stored, proj_seed, offsets):
    width = stored.shape[1]
    param_total = query_grads.shape[1] * 16
    width_total = width * 16
    mine, send = project(proj_seed, offsets, query_grads, width)
    high, low = split_stored(stored)
    part = (mine + lax.ppermute(send, "param", core_swap)).reshape(8, width // 8, 128)
    copies = summed_copies(exchanged(part, "param", chips), param_total, width, width_total)
    own = exchanged(copies, "param", chips)
    other = lax.ppermute(own, "param", core_swap)
    leaving = scores(own, other, high, low, True)
    arrived = [lax.ppermute(x, "proj", y_swap) for x in leaving]
    kept = scores(own, other, high, low, False)
    half = jnp.concatenate([a + b for a, b in zip(kept, arrived)])
    return finish(exchanged(half, "proj", rings), width_total)


def solution(mesh):
    placed = (P(None, "param"), P("param", "proj"), P(), P("param"))
    return jax.shard_map(on_device, mesh=mesh, in_specs=placed, out_specs=P("proj", "param"), check_vma=False)
```
